32 devices in a mesh: gx: 4 (over y, x), gz: 8 (over z, core).
Axes of the slice: x: 2, y: 2, z: 4, core: 2. Of those that a mesh axis runs over, the one named last changes fastest.
Arguments:
- sources: float32 [8, 4, 8, 1280, 128], P('gz', 'gx'), may hold values from -6 to 6
- green: float32 [8, 4, 1280, 1280], P('gz', 'gx'), may hold values from -0.2 to 1.2
- probe: float32 [8, 4, 1024, 1280], P('gz', 'gx'), may hold values from -0.078125 to 0.078125
- batch_pick: int32 [8, 11], replicated, may hold values from 0 to 7
- owner_map: int32 [8, 512], P('gz'), may hold values from 0 to 511, each once within a row
Outputs:
- outgoing: float32 [8, 4, 1280, 1024], P('gz', 'gx')
- receiver_data: float32 [8, 2, 512, 1024], P('gz', None, 'gx')
The draws below stay inside these ranges and needn't reach their ends.
Inputs may be any that keep to these rules, and one draw needn't show every extreme that they name: Each row of owner_map holds every receiver once; slot q belongs to the column q // (512 // 4).
All inputs are finite; a program needn't handle non-finite values.
Results may differ from the reference program's by a relative error of at most 0.00013.
Values sent between devices are 32-bit elements; how exact they have to be, the bound alone decides.
A program may use at most 128 MiB of HBM per device.

```python
import jax
import jax.numpy as jnp
from jax import lax

TRACE = 1280
RECV = 512
SHOTS = 128
SHOTSETS = 8
WINDOW = 8
DIAGS = 11
N_GX = 4
N_GZ = 8


def draw_green(key, part):
    first, second = jax.random.split(key)
    shape = (N_GZ, N_GX, TRACE, TRACE)
    diagonal = jax.random.uniform(first, (N_GZ, N_GX, TRACE), jnp.float32, 0.7, 1.0)
    spread = jax.random.truncated_normal(second, -4.0, 4.0, shape, jnp.float32) * 0.35 / TRACE ** 0.5
    identity = jnp.eye(TRACE, dtype=jnp.float32)
    return spread + diagonal[..., None] * identity


def touch_ends(entries, own_key, low, largest):
    extent = entries.shape
    place = [jax.random.randint(jax.random.fold_in(own_key, axis), (), 0, extent[axis]) for axis in range(len(extent))]
    entries = entries.at[tuple(place)].set(low)
    longest = extent.index(max(extent))
    place[longest] = (place[longest] + 1) % extent[longest]
    return entries.at[tuple(place)].set(largest)


def steps_of(rng, shape, shards, low, top_value):
    gain = 1.0
    for dim, parts in shards:
        steps = jax.random.uniform(jax.random.fold_in(jax.random.fold_in(rng, 6), dim), (parts,), jnp.float32, low / len(shards), top_value / len(shards))
        gain = gain * jnp.repeat(jnp.exp(steps), shape[dim] // parts).reshape((-1,) + (1,) * (len(shape) - 1 - dim))
    return gain


def bell_draw(stream_key, extent, scale, limit, cuts=(), kind=jnp.bfloat16):
    values = scale * jax.random.normal(stream_key, extent, jnp.float32)
    if cuts:
        values = values * steps_of(stream_key, extent, cuts, -0.22, 0.18)
    return jnp.clip(values, -limit, limit).astype(kind)


def setup_inputs(seed: int = 0) -> dict:
    key_list = jax.random.split(jax.random.key(seed), 6)
    return {
        "sources": bell_draw(key_list[0], (N_GZ, N_GX, SHOTSETS, TRACE, SHOTS), 1.0, 6.0, ((0, 8), (1, 4)), jnp.float32),
        "green": draw_green(jax.random.fold_in(key_list[5], 71), 0),
        "probe": bell_draw(key_list[2], (N_GZ, N_GX, 2 * RECV, TRACE), (TRACE * N_GX) ** -0.5, 0.078125, ((0, 8), (1, 4)), jnp.float32),
        "batch_pick": touch_ends(jax.random.randint(key_list[3], (WINDOW, DIAGS), 0, SHOTSETS), jax.random.fold_in(key_list[3], 1), 0, SHOTSETS - 1).astype(jnp.int32),
        "owner_map": jax.vmap(lambda own: jax.random.permutation(own, RECV))(jax.random.split(key_list[4], N_GZ)).reshape((N_GZ, RECV)).astype(jnp.int32),
    }


def reference(sources, green, probe, batch_pick, owner_map):
    columns = WINDOW * SHOTS
    above = [jnp.zeros((TRACE, columns), jnp.float32) for col in range(N_GX)]
    traces_rows = []
    data_rows = []
    for row in range(N_GZ):
        lefter = jnp.zeros((TRACE, columns), jnp.float32)
        current = []
        row_sum = jnp.zeros((2 * RECV, columns), jnp.float32)
        for col in range(N_GX):
            chosen = batch_pick[:, row + col]
            picked = sources[row, col][chosen]
            source = jnp.transpose(picked, (1, 0, 2)).reshape(TRACE, columns)
            inflow = source + 0.5 * (above[col] + lefter)
            result = jnp.dot(green[row, col], inflow, precision=lax.Precision.HIGHEST, preferred_element_type=jnp.float32)
            row_sum = row_sum + jnp.dot(probe[row, col], result, precision=lax.Precision.HIGHEST, preferred_element_type=jnp.float32)
            current.append(result)
            lefter = result
        above = current
        traces_rows.append(jnp.stack(current))
        shaped = row_sum.reshape(2, RECV, columns)
        data_rows.append(jnp.take(shaped, owner_map[row].astype(jnp.int32), axis=1))
    return jnp.stack(traces_rows), jnp.stack(data_rows)
```

```python
import functools

import jax
import jax.numpy as jnp
from jax import lax
from jax.experimental import pallas as pl
from jax.experimental.pallas import tpu as pltpu
from jax.sharding import PartitionSpec as P

MESH = pl.DeviceIdType.MESH
SPLITS = 2
BLOCKS = 2


def divided(value):
    high = value.astype(jnp.bfloat16).astype(jnp.float32)
    return high, value - high


def kernel(
    cols,
    rows,
    pick_ref,
    owner_ref,
    sources_hbm,
    green_hbm,
    probe_hbm,
    traces_hbm,
    data_hbm,
    sources,
    staging,
    operator,
    receive_map,
    inflow,
    stacked,
    wide,
    traces,
    outbox,
    upper,
    lefter,
    partial,
    *rest,
):
    stages = cols.bit_length() - 1
    arrivals = rest[:stages]
    (
        green_sem,
        sources_sem,
        probe_sem,
        down_sem,
        right_sem,
        upper_sem,
        lefter_sem,
        traces_sem,
        data_sem,
        sum_send_sem,
        sum_recv_sem,
    ) = rest[stages:]
    row = lax.axis_index("gz")
    col = lax.axis_index("gx")
    diag = row + col
    trace = green_hbm.shape[0]
    shots = sources_hbm.shape[2]
    window = pick_ref.shape[0]
    half = trace // SPLITS
    piece = half // BLOCKS
    share = shots // SPLITS
    receivers = owner_ref.shape[1]
    owned = receivers // cols

    loads = []
    for block in range(BLOCKS):
        for side in range(SPLITS):
            where = pl.ds(side * half + block * piece, piece)
            loads.append(
                pltpu.make_async_copy(
                    green_hbm.at[where], staging.at[where], green_sem.at[block * SPLITS + side]
                )
            )
    for load in loads:
        load.start()
    sources_load = pltpu.make_async_copy(sources_hbm, sources, sources_sem)
    sources_load.start()

    partners = [col ^ (cols >> (stage + 1)) for stage in range(stages)]
    barrier = pltpu.get_barrier_semaphore()

    @pl.when(row > 0)
    def _():
        pl.semaphore_signal(barrier, inc=1, device_id={"gz": row - 1}, device_id_type=MESH)

    @pl.when(row < rows - 1)
    def _():
        pl.semaphore_signal(barrier, inc=1, device_id={"gz": row + 1}, device_id_type=MESH)

    for offset in range(1, cols):
        other = lax.rem(col + offset, cols)
        pl.semaphore_signal(barrier, inc=1, device_id={"gx": other}, device_id_type=MESH)

    for block in range(BLOCKS):
        for side in range(SPLITS):
            loads[block * SPLITS + side].wait()
            high, low = divided(staging[pl.ds(side * half + block * piece, piece), :])
            place = pl.ds((block * SPLITS + side) * piece, piece)
            operator[place, :trace] = high.astype(jnp.bfloat16)
            operator[place, trace:] = low.astype(jnp.bfloat16)
    probe_load = pltpu.make_async_copy(
        probe_hbm, staging.at[pl.ds(0, SPLITS * receivers)], probe_sem
    )
    probe_load.start()
    sources_load.wait()

    peers = cols - 1 + (row > 0).astype(jnp.int32) + (row < rows - 1).astype(jnp.int32)
    pl.semaphore_wait(barrier, peers)

    def downward(slot, part):
        return pltpu.make_async_remote_copy(
            src_ref=outbox.at[slot, part],
            dst_ref=upper.at[slot, part],
            send_sem=down_sem.at[slot],
            recv_sem=upper_sem.at[slot],
            device_id={"gz": lax.rem(row + 1, rows)},
            device_id_type=MESH,
        )

    def rightward(slot, part):
        return pltpu.make_async_remote_copy(
            src_ref=outbox.at[slot, part],
            dst_ref=lefter.at[slot, part],
            send_sem=right_sem.at[slot],
            recv_sem=lefter_sem.at[slot],
            device_id={"gx": lax.rem(col + 1, cols)},
            device_id_type=MESH,
        )

    whole = pl.ds(0, half)
    first_lanes = lax.broadcasted_iota(jnp.int32, (half, shots), 1) < share
    piece_lanes = lax.broadcasted_iota(jnp.int32, (piece, shots), 1) < share
    last = window * SPLITS - 1

    def chunk(batch, part):
        slot = batch * SPLITS + part
        chosen = pick_ref[batch, diag]
        top = sources[chosen, :half, :]
        bottom = sources[chosen, half:, :]
        if part == 0:
            inflow[...] = jnp.where(first_lanes, top, pltpu.roll(bottom, share, 1))
        else:
            inflow[...] = jnp.where(first_lanes, pltpu.roll(top, share, 1), bottom)

        @pl.when(row > 0)
        def _():
            downward(slot, whole).wait_recv()
            inflow[...] += 0.5 * upper[slot]

        @pl.when(col > 0)
        def _():
            rightward(slot, whole).wait_recv()
            inflow[...] += 0.5 * lefter[slot]

        high, low = divided(inflow[...])
        top = jnp.where(first_lanes, high, pltpu.roll(low, share, 1)).astype(jnp.bfloat16)
        bottom = jnp.where(first_lanes, pltpu.roll(high, share, 1), low).astype(jnp.bfloat16)
        for copy in range(2):
            stacked[copy * trace : copy * trace + half, :] = top
            stacked[copy * trace + half : (copy + 1) * trace, :] = bottom
        for block in range(BLOCKS):
            result = jnp.dot(
                operator[block * SPLITS * piece : (block + 1) * SPLITS * piece, :],
                stacked[...],
                preferred_element_type=jnp.float32,
            )
            result = result + pltpu.roll(result, share, 1)
            upside, downside = result[:piece], result[piece:]
            area = pl.ds(block * piece, piece)
            outbox[slot, area, :] = jnp.where(piece_lanes, upside, downside)

            @pl.when(row < rows - 1)
            def _():
                downward(slot, area).start()

            @pl.when(col < cols - 1)
            def _():
                rightward(slot, area).start()

            for side, value in ((0, upside), (1, downside)):
                begin = side * half + block * piece
                if part > 0:
                    value = jnp.where(piece_lanes, traces[batch, begin : begin + piece, :], value)
                traces[batch, begin : begin + piece, :] = value

    def traces_out(batch):
        return pltpu.make_async_copy(
            traces.at[batch],
            traces_hbm.at[:, pl.ds(pl.multiple_of(batch * shots, shots), shots)],
            traces_sem.at[batch],
        )

    def arrange_map():
        probe_load.wait()
        spots = lax.broadcasted_iota(jnp.int32, (receivers, receivers), 0)
        chosen = (spots == owner_ref[...]).astype(jnp.float32)
        chosen = jnp.transpose(chosen).astype(jnp.bfloat16)
        for part in range(2):
            values = staging[part * receivers : (part + 1) * receivers, :]
            for index, value in enumerate(divided(values)):
                moved = jnp.dot(
                    chosen, value.astype(jnp.bfloat16), preferred_element_type=jnp.float32
                ).astype(jnp.bfloat16)
                for owner in range(cols):
                    begin = (owner * 2 + part) * owned
                    receive_map[begin : begin + owned, index * trace : (index + 1) * trace] = moved[
                        owner * owned : (owner + 1) * owned
                    ]

    def measure(batch):
        high, low = divided(traces[batch])
        for copy in range(2):
            wide[copy * trace : (copy + 1) * trace, :shots] = high.astype(jnp.bfloat16)
            wide[copy * trace : (copy + 1) * trace, shots:] = low.astype(jnp.bfloat16)
        for side in range(2):
            value = jnp.dot(
                receive_map[side * receivers : (side + 1) * receivers, :],
                wide[...],
                preferred_element_type=jnp.float32,
            )
            partial[batch, side * receivers : (side + 1) * receivers, :] = (
                value[:, :shots] + value[:, shots:]
            )

    def exchange(stage, batch):
        extent = (cols >> (stage + 1)) * 2 * owned
        base = (col // (cols >> stage)) * (cols >> stage) * 2 * owned
        upside = (col // (cols >> (stage + 1))) % 2
        mine = pl.multiple_of(base + upside * extent, 2 * owned)
        theirs = pl.multiple_of(base + (1 - upside) * extent, 2 * owned)
        copy = pltpu.make_async_remote_copy(
            src_ref=partial.at[batch, pl.ds(theirs, extent)],
            dst_ref=arrivals[stage].at[batch],
            send_sem=sum_send_sem.at[stage, batch],
            recv_sem=sum_recv_sem.at[stage, batch],
            device_id={"gx": partners[stage]},
            device_id_type=MESH,
        )
        return copy, pl.ds(mine, extent)

    def data_out(batch, part):
        begin = pl.multiple_of(col * 2 * owned + part * owned, owned)
        return pltpu.make_async_copy(
            partial.at[batch, pl.ds(begin, owned)],
            data_hbm.at[part, :, pl.ds(pl.multiple_of(batch * shots, shots), shots)],
            data_sem.at[batch, part],
        )

    lags = []
    lag = 0
    longest = 0
    for stage in range(stages):
        distance = cols >> (stage + 1)
        upside = (col // distance) % 2
        lag = lag + (1 - upside) * ((distance + 2) // 2)
        longest += (distance + 2) // 2
        lags.append(lag)

    def advance(step, carry):
        @pl.when(step < window)
        def _():
            for part in range(SPLITS):
                chunk(step, part)
            traces_out(step).start()

            @pl.when(step == 0)
            def _():
                arrange_map()

            measure(step)
            exchange(0, step)[0].start()

        for stage in range(stages):
            batch = step - lags[stage]

            @pl.when(jnp.logical_and(batch >= 0, batch < window))
            def _():
                copy, mine = exchange(stage, batch)
                copy.wait_recv()
                partial[batch, mine, :] += arrivals[stage][batch]
                if stage < stages - 1:
                    exchange(stage + 1, batch)[0].start()
                else:
                    for part in range(2):
                        data_out(batch, part).start()

        return carry

    lax.fori_loop(0, window + longest, advance, 0)

    def finish(batch, carry):
        for part in range(SPLITS):
            slot = batch * SPLITS + part

            @pl.when(row < rows - 1)
            def _():
                downward(slot, whole).wait_send()

            @pl.when(col < cols - 1)
            def _():
                rightward(slot, whole).wait_send()

        for stage in range(stages):
            exchange(stage, batch)[0].wait_send()
        traces_out(batch).wait()
        for part in range(2):
            data_out(batch, part).wait()
        return carry

    lax.fori_loop(0, window, finish, 0)


def local(sources, green, probe, batch_pick, owner_map):
    cols = lax.axis_size("gx")
    rows = lax.axis_size("gz")
    batches, trace, shots = sources.shape[2:]
    window = batch_pick.shape[0]
    receivers = owner_map.shape[1]
    owned = receivers // cols
    stages = cols.bit_length() - 1
    slots = window * SPLITS
    half = trace // SPLITS
    total = window * shots
    vmem = pltpu.VMEM
    dma = pltpu.SemaphoreType.DMA
    anywhere = pl.BlockSpec(memory_space=pl.ANY)
    traces, data = pl.pallas_call(
        functools.partial(kernel, cols, rows),
        out_shape=(
            jax.ShapeDtypeStruct((trace, total), jnp.float32),
            jax.ShapeDtypeStruct((2, owned, total), jnp.float32),
        ),
        in_specs=[
            pl.BlockSpec(memory_space=pltpu.SMEM),
            pl.BlockSpec(memory_space=pltpu.VMEM),
            anywhere,
            anywhere,
            anywhere,
        ],
        out_specs=(anywhere, anywhere),
        scratch_shapes=[
            vmem((batches, trace, shots), jnp.float32),
            vmem((max(trace, 2 * receivers), trace), jnp.float32),
            vmem((trace, 2 * trace), jnp.bfloat16),
            vmem((2 * receivers, 2 * trace), jnp.bfloat16),
            vmem((half, shots), jnp.float32),
            vmem((2 * trace, shots), jnp.bfloat16),
            vmem((2 * trace, 2 * shots), jnp.bfloat16),
            vmem((window, trace, shots), jnp.float32),
            vmem((slots, half, shots), jnp.float32),
            vmem((slots, half, shots), jnp.float32),
            vmem((slots, half, shots), jnp.float32),
            vmem((window, 2 * receivers, shots), jnp.float32),
        ]
        + [
            vmem((window, (cols >> (stage + 1)) * 2 * owned, shots), jnp.float32)
            for stage in range(stages)
        ]
        + [
            dma((SPLITS * BLOCKS,)),
            dma(()),
            dma(()),
            dma((slots,)),
            dma((slots,)),
            dma((slots,)),
            dma((slots,)),
            dma((window,)),
            dma((window, 2)),
            dma((stages, window)),
            dma((stages, window)),
        ],
        compiler_params=pltpu.CompilerParams(
            collective_id=0, has_side_effects=True, vmem_limit_bytes=67043328
        ),
    )(batch_pick, owner_map, sources[0, 0], green[0, 0], probe[0, 0])
    return traces[None, None], data[None]


def solution(mesh):
    return jax.shard_map(
        local,
        mesh=mesh,
        in_specs=(
            P("gz", "gx", None, None, None),
            P("gz", "gx", None, None),
            P("gz", "gx", None, None),
            P(),
            P("gz", None),
        ),
        out_specs=(P("gz", "gx", None, None), P("gz", None, "gx", None)),
        check_vma=False,
    )
```

```python
import functools

import jax
import jax.numpy as jnp
from jax import lax
from jax.experimental import pallas as pl
from jax.experimental.pallas import tpu as pltpu
from jax.sharding import PartitionSpec as P

MESH = pl.DeviceIdType.MESH
SPLITS = 2
BLOCKS = 4


def divided(value):
    high = value.astype(jnp.bfloat16).astype(jnp.float32)
    return high, value - high


def kernel(
    cols,
    rows,
    pick_ref,
    owner_ref,
    sources_hbm,
    green_hbm,
    probe_hbm,
    traces_hbm,
    data_hbm,
    sources,
    staging,
    operator,
    receive_map,
    inflow,
    stacked,
    wide,
    traces,
    outbox,
    upper,
    lefter,
    partial,
    *rest,
):
    group = cols // 2
    stages = group.bit_length() - 1
    crossed = rest[:2]
    arrivals = (rest[2 : 2 + stages], rest[2 + stages : 2 + 2 * stages])
    (
        green_sem,
        sources_sem,
        probe_sem,
        down_sem,
        right_sem,
        upper_sem,
        lefter_sem,
        traces_sem,
        data_sem,
        cross_send_sem,
        cross_recv_sem,
        sum_send_sem,
        sum_recv_sem,
    ) = rest[2 + 2 * stages :]
    row = lax.axis_index("gz")
    col = lax.axis_index("gx")
    diag = row + col
    trace = green_hbm.shape[0]
    shots = sources_hbm.shape[2]
    window = pick_ref.shape[0]
    half = trace // SPLITS
    piece = half // BLOCKS
    share = shots // SPLITS
    receivers = owner_ref.shape[1]
    owned = receivers // cols

    loads = []
    for block in range(BLOCKS):
        for side in range(SPLITS):
            where = pl.ds(side * half + block * piece, piece)
            loads.append(
                pltpu.make_async_copy(
                    green_hbm.at[where], staging.at[where], green_sem.at[block * SPLITS + side]
                )
            )
    for load in loads:
        load.start()
    sources_load = pltpu.make_async_copy(sources_hbm, sources, sources_sem)
    sources_load.start()

    barrier = pltpu.get_barrier_semaphore()

    @pl.when(row > 0)
    def _():
        pl.semaphore_signal(barrier, inc=1, device_id={"gz": row - 1}, device_id_type=MESH)

    @pl.when(row < rows - 1)
    def _():
        pl.semaphore_signal(barrier, inc=1, device_id={"gz": row + 1}, device_id_type=MESH)

    for offset in range(1, cols):
        other = lax.rem(col + offset, cols)
        pl.semaphore_signal(barrier, inc=1, device_id={"gx": other}, device_id_type=MESH)

    for block in range(BLOCKS):
        for side in range(SPLITS):
            loads[block * SPLITS + side].wait()
            high, low = divided(staging[pl.ds(side * half + block * piece, piece), :])
            place = pl.ds((block * SPLITS + side) * piece, piece)
            operator[place, :trace] = high.astype(jnp.bfloat16)
            operator[place, trace:] = low.astype(jnp.bfloat16)
    probe_load = pltpu.make_async_copy(
        probe_hbm, staging.at[pl.ds(0, SPLITS * receivers)], probe_sem
    )
    probe_load.start()
    sources_load.wait()

    peers = cols - 1 + (row > 0).astype(jnp.int32) + (row < rows - 1).astype(jnp.int32)
    pl.semaphore_wait(barrier, peers)

    def downward(slot, part):
        return pltpu.make_async_remote_copy(
            src_ref=outbox.at[slot, part],
            dst_ref=upper.at[slot, part],
            send_sem=down_sem.at[slot],
            recv_sem=upper_sem.at[slot],
            device_id={"gz": lax.rem(row + 1, rows)},
            device_id_type=MESH,
        )

    def rightward(slot, part):
        return pltpu.make_async_remote_copy(
            src_ref=outbox.at[slot, part],
            dst_ref=lefter.at[slot, part],
            send_sem=right_sem.at[slot],
            recv_sem=lefter_sem.at[slot],
            device_id={"gx": lax.rem(col + 1, cols)},
            device_id_type=MESH,
        )

    whole = pl.ds(0, half)
    first_lanes = lax.broadcasted_iota(jnp.int32, (half, shots), 1) < share
    piece_lanes = lax.broadcasted_iota(jnp.int32, (piece, shots), 1) < share
    last = window * SPLITS - 1

    def chunk(batch, part):
        slot = batch * SPLITS + part
        chosen = pick_ref[batch, diag]
        top = sources[chosen, :half, :]
        bottom = sources[chosen, half:, :]
        if part == 0:
            inflow[...] = jnp.where(first_lanes, top, pltpu.roll(bottom, share, 1))
        else:
            inflow[...] = jnp.where(first_lanes, pltpu.roll(top, share, 1), bottom)

        @pl.when(row > 0)
        def _():
            downward(slot, whole).wait_recv()
            inflow[...] += 0.5 * upper[slot]

        @pl.when(col > 0)
        def _():
            rightward(slot, whole).wait_recv()
            inflow[...] += 0.5 * lefter[slot]

        high, low = divided(inflow[...])
        top = jnp.where(first_lanes, high, pltpu.roll(low, share, 1)).astype(jnp.bfloat16)
        bottom = jnp.where(first_lanes, pltpu.roll(high, share, 1), low).astype(jnp.bfloat16)
        for copy in range(2):
            stacked[copy * trace : copy * trace + half, :] = top
            stacked[copy * trace + half : (copy + 1) * trace, :] = bottom
        for block in range(BLOCKS):
            result = jnp.dot(
                operator[block * SPLITS * piece : (block + 1) * SPLITS * piece, :],
                stacked[...],
                preferred_element_type=jnp.float32,
            )
            result = result + pltpu.roll(result, share, 1)
            upside, downside = result[:piece], result[piece:]
            area = pl.ds(block * piece, piece)
            outbox[slot, area, :] = jnp.where(piece_lanes, upside, downside)

            @pl.when(row < rows - 1)
            def _():
                downward(slot, area).start()

            @pl.when(col < cols - 1)
            def _():
                rightward(slot, area).start()

            for side, value in ((0, upside), (1, downside)):
                begin = side * half + block * piece
                if part > 0:
                    value = jnp.where(piece_lanes, traces[batch, begin : begin + piece, :], value)
                traces[batch, begin : begin + piece, :] = value

    def traces_out(batch):
        return pltpu.make_async_copy(
            traces.at[batch],
            traces_hbm.at[:, pl.ds(pl.multiple_of(batch * shots, shots), shots)],
            traces_sem.at[batch],
        )

    def arrange_map():
        probe_load.wait()
        spots = lax.broadcasted_iota(jnp.int32, (receivers, receivers), 0)
        chosen = (spots == owner_ref[...]).astype(jnp.float32)
        chosen = jnp.transpose(chosen).astype(jnp.bfloat16)
        for part in range(2):
            values = staging[part * receivers : (part + 1) * receivers, :]
            for index, value in enumerate(divided(values)):
                moved = jnp.dot(
                    chosen, value.astype(jnp.bfloat16), preferred_element_type=jnp.float32
                ).astype(jnp.bfloat16)
                for owner in range(cols):
                    begin = (owner * 2 + part) * owned
                    receive_map[begin : begin + owned, index * trace : (index + 1) * trace] = moved[
                        owner * owned : (owner + 1) * owned
                    ]

    def measure(batch):
        high, low = divided(traces[batch])
        for copy in range(2):
            wide[copy * trace : (copy + 1) * trace, :shots] = high.astype(jnp.bfloat16)
            wide[copy * trace : (copy + 1) * trace, shots:] = low.astype(jnp.bfloat16)
        for side in range(2):
            value = jnp.dot(
                receive_map[side * receivers : (side + 1) * receivers, :],
                wide[...],
                preferred_element_type=jnp.float32,
            )
            partial[batch, side * receivers : (side + 1) * receivers, :] = (
                value[:, :shots] + value[:, shots:]
            )

    unit = 2 * owned
    upside = col // group
    place = lax.rem(col, group)

    def cross(kind, batch):
        if kind == 0:
            area = pl.ds(0, group * unit)
        else:
            area = pl.ds(pl.multiple_of((group + place) * unit, unit), unit)
        copy = pltpu.make_async_remote_copy(
            src_ref=partial.at[batch, area],
            dst_ref=crossed[kind].at[batch],
            send_sem=cross_send_sem.at[kind, batch],
            recv_sem=cross_recv_sem.at[kind, batch],
            device_id={"gx": lax.rem(col + group, cols)},
            device_id_type=MESH,
        )
        return copy, area

    def exchange(kind, stage, batch):
        distance = group >> (stage + 1)
        base = kind * group + (place // (2 * distance)) * (2 * distance)
        bit = lax.rem(place // distance, 2)
        mine = pl.multiple_of((base + bit * distance) * unit, unit)
        theirs = pl.multiple_of((base + (1 - bit) * distance) * unit, unit)
        copy = pltpu.make_async_remote_copy(
            src_ref=partial.at[batch, pl.ds(theirs, distance * unit)],
            dst_ref=arrivals[kind][stage].at[batch],
            send_sem=sum_send_sem.at[kind, stage, batch],
            recv_sem=sum_recv_sem.at[kind, stage, batch],
            device_id={"gx": col + (1 - 2 * bit) * distance},
            device_id_type=MESH,
        )
        return copy, pl.ds(mine, distance * unit)

    def data_out(batch, part):
        begin = pl.multiple_of(col * 2 * owned + part * owned, owned)
        return pltpu.make_async_copy(
            partial.at[batch, pl.ds(begin, owned)],
            data_hbm.at[part, :, pl.ds(pl.multiple_of(batch * shots, shots), shots)],
            data_sem.at[batch, part],
        )

    def advance(step, carry):
        @pl.when(step < window)
        def _():
            for part in range(SPLITS):
                chunk(step, part)
            traces_out(step).start()

            @pl.when(step == 0)
            def _():
                arrange_map()

            measure(step)

            @pl.when(upside == 1)
            def _():
                cross(0, step)[0].start()

        def sum_out(batch):
            for part in range(2):
                data_out(batch, part).start()

        def follow(kind, stage, batch):
            if stage < stages:
                exchange(kind, stage, batch)[0].start()
            elif kind == 0:
                sum_out(batch)
            else:

                @pl.when(upside == 0)
                def _():
                    cross(1, batch)[0].start()

        def collect(kind, stage, batch):
            copy, mine = exchange(kind, stage, batch)
            copy.wait_recv()
            partial[batch, mine, :] += arrivals[kind][stage][batch]
            follow(kind, stage + 1, batch)

        @pl.when(step == window)
        def _():
            lax.fori_loop(0, window, lambda batch, none: (follow(1, 0, batch), none)[1], 0)

        def within(batch, *more):
            known = jnp.logical_and(batch >= 0, batch < window)
            for condition in more:
                known = jnp.logical_and(known, condition)
            return known

        early = step - window

        @pl.when(within(early, upside == 0))
        def _():
            copy, area = cross(0, early)
            copy.wait_recv()
            partial[early, area, :] += crossed[0][early]
            follow(0, 0, early)

        for stage in range(stages):
            batch = step - window - 2 - stage

            @pl.when(within(batch))
            def _():
                collect(1, stage, batch)

            @pl.when(within(batch, upside == 0))
            def _():
                collect(0, stage, batch)

        late = step - window - 3 - stages

        @pl.when(within(late, upside == 1))
        def _():
            copy, area = cross(1, late)
            copy.wait_recv()
            partial[late, area, :] += crossed[1][late]
            sum_out(late)

        return carry

    lax.fori_loop(0, 2 * window + stages + 3, advance, 0)

    def finish(batch, carry):
        for part in range(SPLITS):
            slot = batch * SPLITS + part

            @pl.when(row < rows - 1)
            def _():
                downward(slot, whole).wait_send()

            @pl.when(col < cols - 1)
            def _():
                rightward(slot, whole).wait_send()

        @pl.when(upside == 1)
        def _():
            cross(0, batch)[0].wait_send()

        @pl.when(upside == 0)
        def _():
            cross(1, batch)[0].wait_send()
            for stage in range(stages):
                exchange(0, stage, batch)[0].wait_send()

        for stage in range(stages):
            exchange(1, stage, batch)[0].wait_send()
        traces_out(batch).wait()
        for part in range(2):
            data_out(batch, part).wait()
        return carry

    lax.fori_loop(0, window, finish, 0)


def local(sources, green, probe, batch_pick, owner_map):
    cols = lax.axis_size("gx")
    rows = lax.axis_size("gz")
    batches, trace, shots = sources.shape[2:]
    window = batch_pick.shape[0]
    receivers = owner_map.shape[1]
    owned = receivers // cols
    group = cols // 2
    stages = group.bit_length() - 1
    slots = window * SPLITS
    half = trace // SPLITS
    total = window * shots
    vmem = pltpu.VMEM
    dma = pltpu.SemaphoreType.DMA
    anywhere = pl.BlockSpec(memory_space=pl.ANY)
    traces, data = pl.pallas_call(
        functools.partial(kernel, cols, rows),
        out_shape=(
            jax.ShapeDtypeStruct((trace, total), jnp.float32),
            jax.ShapeDtypeStruct((2, owned, total), jnp.float32),
        ),
        in_specs=[
            pl.BlockSpec(memory_space=pltpu.SMEM),
            pl.BlockSpec(memory_space=pltpu.VMEM),
            anywhere,
            anywhere,
            anywhere,
        ],
        out_specs=(anywhere, anywhere),
        scratch_shapes=[
            vmem((batches, trace, shots), jnp.float32),
            vmem((max(trace, 2 * receivers), trace), jnp.float32),
            vmem((trace, 2 * trace), jnp.bfloat16),
            vmem((2 * receivers, 2 * trace), jnp.bfloat16),
            vmem((half, shots), jnp.float32),
            vmem((2 * trace, shots), jnp.bfloat16),
            vmem((2 * trace, 2 * shots), jnp.bfloat16),
            vmem((window, trace, shots), jnp.float32),
            vmem((slots, half, shots), jnp.float32),
            vmem((slots, half, shots), jnp.float32),
            vmem((slots, half, shots), jnp.float32),
            vmem((window, 2 * receivers, shots), jnp.float32),
        ]
        + [
            vmem((window, group * 2 * owned, shots), jnp.float32),
            vmem((window, 2 * owned, shots), jnp.float32),
        ]
        + [
            vmem((window, (group >> (stage + 1)) * 2 * owned, shots), jnp.float32)
            for kind in range(2)
            for stage in range(stages)
        ]
        + [
            dma((SPLITS * BLOCKS,)),
            dma(()),
            dma(()),
            dma((slots,)),
            dma((slots,)),
            dma((slots,)),
            dma((slots,)),
            dma((window,)),
            dma((window, 2)),
            dma((2, window)),
            dma((2, window)),
            dma((2, max(stages, 1), window)),
            dma((2, max(stages, 1), window)),
        ],
        compiler_params=pltpu.CompilerParams(
            collective_id=0, has_side_effects=True, vmem_limit_bytes=67043328
        ),
    )(batch_pick, owner_map, sources[0, 0], green[0, 0], probe[0, 0])
    return traces[None, None], data[None]


def solution(mesh):
    return jax.shard_map(
        local,
        mesh=mesh,
        in_specs=(
            P("gz", "gx", None, None, None),
            P("gz", "gx", None, None),
            P("gz", "gx", None, None),
            P(),
            P("gz", None),
        ),
        out_specs=(P("gz", "gx", None, None), P("gz", None, "gx", None)),
        check_vma=False,
    )
```

```python
import functools

import jax
import jax.numpy as jnp
from jax import lax
from jax.experimental import pallas as pl
from jax.experimental.pallas import tpu as pltpu
from jax.sharding import PartitionSpec as P

MESH = pl.DeviceIdType.MESH
SPLITS = 2
BLOCKS = 4


def divided(value):
    high = value.astype(jnp.bfloat16).astype(jnp.float32)
    return high, value - high


def kernel(
    cols,
    rows,
    pick_ref,
    owner_ref,
    sources_hbm,
    green_hbm,
    probe_hbm,
    traces_hbm,
    data_hbm,
    sources,
    staging,
    operator,
    receive_map,
    inflow,
    stacked,
    wide,
    traces,
    outbox,
    upper,
    lefter,
    partial,
    *rest,
):
    group = cols // 2
    stages = group.bit_length() - 1
    crossed = rest[:2]
    arrivals = (rest[2 : 2 + stages], rest[2 + stages : 2 + 2 * stages])
    (
        green_sem,
        sources_sem,
        probe_sem,
        down_sem,
        right_sem,
        upper_sem,
        lefter_sem,
        traces_sem,
        data_sem,
        cross_send_sem,
        cross_recv_sem,
        sum_send_sem,
        sum_recv_sem,
    ) = rest[2 + 2 * stages :]
    row = lax.axis_index("gz")
    col = lax.axis_index("gx")
    diag = row + col
    trace = green_hbm.shape[0]
    shots = sources_hbm.shape[2]
    window = pick_ref.shape[0]
    half = trace // SPLITS
    piece = half // BLOCKS
    share = shots // SPLITS
    receivers = owner_ref.shape[1]
    owned = receivers // cols

    loads = []
    for block in range(BLOCKS):
        for side in range(SPLITS):
            where = pl.ds(side * half + block * piece, piece)
            loads.append(
                pltpu.make_async_copy(
                    green_hbm.at[where], staging.at[where], green_sem.at[block * SPLITS + side]
                )
            )
    for load in loads:
        load.start()
    sources_load = pltpu.make_async_copy(sources_hbm, sources, sources_sem)
    sources_load.start()

    barrier = pltpu.get_barrier_semaphore()

    @pl.when(row > 0)
    def _():
        pl.semaphore_signal(barrier, inc=1, device_id={"gz": row - 1}, device_id_type=MESH)

    @pl.when(row < rows - 1)
    def _():
        pl.semaphore_signal(barrier, inc=1, device_id={"gz": row + 1}, device_id_type=MESH)

    for offset in range(1, cols):
        other = lax.rem(col + offset, cols)
        pl.semaphore_signal(barrier, inc=1, device_id={"gx": other}, device_id_type=MESH)

    for block in range(BLOCKS):
        for side in range(SPLITS):
            loads[block * SPLITS + side].wait()
            high, low = divided(staging[pl.ds(side * half + block * piece, piece), :])
            place = pl.ds((block * SPLITS + side) * piece, piece)
            operator[place, :trace] = high.astype(jnp.bfloat16)
            operator[place, trace:] = low.astype(jnp.bfloat16)
    probe_load = pltpu.make_async_copy(
        probe_hbm, staging.at[pl.ds(0, SPLITS * receivers)], probe_sem
    )
    probe_load.start()
    sources_load.wait()

    peers = cols - 1 + (row > 0).astype(jnp.int32) + (row < rows - 1).astype(jnp.int32)
    pl.semaphore_wait(barrier, peers)

    def downward(slot, part):
        return pltpu.make_async_remote_copy(
            src_ref=outbox.at[slot, part],
            dst_ref=upper.at[slot, part],
            send_sem=down_sem.at[slot],
            recv_sem=upper_sem.at[slot],
            device_id={"gz": lax.rem(row + 1, rows)},
            device_id_type=MESH,
        )

    def rightward(slot, part):
        return pltpu.make_async_remote_copy(
            src_ref=outbox.at[slot, part],
            dst_ref=lefter.at[slot, part],
            send_sem=right_sem.at[slot],
            recv_sem=lefter_sem.at[slot],
            device_id={"gx": lax.rem(col + 1, cols)},
            device_id_type=MESH,
        )

    whole = pl.ds(0, half)
    first_lanes = lax.broadcasted_iota(jnp.int32, (half, shots), 1) < share
    piece_lanes = lax.broadcasted_iota(jnp.int32, (piece, shots), 1) < share
    last = window * SPLITS - 1

    def chunk(batch, part):
        slot = batch * SPLITS + part
        chosen = pick_ref[batch, diag]
        top = sources[chosen, :half, :]
        bottom = sources[chosen, half:, :]
        if part == 0:
            inflow[...] = jnp.where(first_lanes, top, pltpu.roll(bottom, share, 1))
        else:
            inflow[...] = jnp.where(first_lanes, pltpu.roll(top, share, 1), bottom)

        @pl.when(row > 0)
        def _():
            downward(slot, whole).wait_recv()
            inflow[...] += 0.5 * upper[slot]

        @pl.when(col > 0)
        def _():
            rightward(slot, whole).wait_recv()
            inflow[...] += 0.5 * lefter[slot]

        high, low = divided(inflow[...])
        top = jnp.where(first_lanes, high, pltpu.roll(low, share, 1)).astype(jnp.bfloat16)
        bottom = jnp.where(first_lanes, pltpu.roll(high, share, 1), low).astype(jnp.bfloat16)
        for copy in range(2):
            stacked[copy * trace : copy * trace + half, :] = top
            stacked[copy * trace + half : (copy + 1) * trace, :] = bottom
        for block in range(BLOCKS):
            lines = slice(block * SPLITS * piece, (block + 1) * SPLITS * piece)
            result = 0.0
            for begin in range(0, 2 * trace, half):
                result = result + jnp.dot(
                    operator[lines, begin : begin + half],
                    stacked[begin : begin + half],
                    preferred_element_type=jnp.float32,
                )
            result = result + pltpu.roll(result, share, 1)
            upside, downside = result[:piece], result[piece:]
            area = pl.ds(block * piece, piece)
            outbox[slot, area, :] = jnp.where(piece_lanes, upside, downside)

            @pl.when(row < rows - 1)
            def _():
                downward(slot, area).start()

            @pl.when(col < cols - 1)
            def _():
                rightward(slot, area).start()

            for side, value in ((0, upside), (1, downside)):
                begin = side * half + block * piece
                if part > 0:
                    value = jnp.where(piece_lanes, traces[batch, begin : begin + piece, :], value)
                traces[batch, begin : begin + piece, :] = value

    def traces_out(batch):
        return pltpu.make_async_copy(
            traces.at[batch],
            traces_hbm.at[:, pl.ds(pl.multiple_of(batch * shots, shots), shots)],
            traces_sem.at[batch],
        )

    def arrange_map():
        probe_load.wait()
        spots = lax.broadcasted_iota(jnp.int32, (receivers, receivers), 0)
        chosen = (spots == owner_ref[...]).astype(jnp.float32)
        chosen = jnp.transpose(chosen).astype(jnp.bfloat16)
        for part in range(2):
            values = staging[part * receivers : (part + 1) * receivers, :]
            for index, value in enumerate(divided(values)):
                moved = jnp.dot(
                    chosen, value.astype(jnp.bfloat16), preferred_element_type=jnp.float32
                ).astype(jnp.bfloat16)
                for owner in range(cols):
                    begin = (owner * 2 + part) * owned
                    receive_map[begin : begin + owned, index * trace : (index + 1) * trace] = moved[
                        owner * owned : (owner + 1) * owned
                    ]

    def measure(batch):
        high, low = divided(traces[batch])
        for copy in range(2):
            wide[copy * trace : (copy + 1) * trace, :shots] = high.astype(jnp.bfloat16)
            wide[copy * trace : (copy + 1) * trace, shots:] = low.astype(jnp.bfloat16)
        for side in range(2):
            value = jnp.dot(
                receive_map[side * receivers : (side + 1) * receivers, :],
                wide[...],
                preferred_element_type=jnp.float32,
            )
            partial[batch, side * receivers : (side + 1) * receivers, :] = (
                value[:, :shots] + value[:, shots:]
            )

    unit = 2 * owned
    upside = col // group
    place = lax.rem(col, group)

    def cross(kind, batch):
        if kind == 0:
            area = pl.ds(0, group * unit)
        else:
            area = pl.ds(pl.multiple_of((group + place) * unit, unit), unit)
        copy = pltpu.make_async_remote_copy(
            src_ref=partial.at[batch, area],
            dst_ref=crossed[kind].at[batch],
            send_sem=cross_send_sem.at[kind, batch],
            recv_sem=cross_recv_sem.at[kind, batch],
            device_id={"gx": lax.rem(col + group, cols)},
            device_id_type=MESH,
        )
        return copy, area

    def exchange(kind, stage, batch):
        distance = group >> (stage + 1)
        base = kind * group + (place // (2 * distance)) * (2 * distance)
        bit = lax.rem(place // distance, 2)
        mine = pl.multiple_of((base + bit * distance) * unit, unit)
        theirs = pl.multiple_of((base + (1 - bit) * distance) * unit, unit)
        copy = pltpu.make_async_remote_copy(
            src_ref=partial.at[batch, pl.ds(theirs, distance * unit)],
            dst_ref=arrivals[kind][stage].at[batch],
            send_sem=sum_send_sem.at[kind, stage, batch],
            recv_sem=sum_recv_sem.at[kind, stage, batch],
            device_id={"gx": col + (1 - 2 * bit) * distance},
            device_id_type=MESH,
        )
        return copy, pl.ds(mine, distance * unit)

    def data_out(batch, part):
        begin = pl.multiple_of(col * 2 * owned + part * owned, owned)
        return pltpu.make_async_copy(
            partial.at[batch, pl.ds(begin, owned)],
            data_hbm.at[part, :, pl.ds(pl.multiple_of(batch * shots, shots), shots)],
            data_sem.at[batch, part],
        )

    def advance(step, carry):
        @pl.when(step < window)
        def _():
            for part in range(SPLITS):
                chunk(step, part)
            traces_out(step).start()

            @pl.when(step == 0)
            def _():
                arrange_map()

            measure(step)

            @pl.when(upside == 1)
            def _():
                cross(0, step)[0].start()

        def sum_out(batch):
            for part in range(2):
                data_out(batch, part).start()

        def follow(kind, stage, batch):
            if stage < stages:
                exchange(kind, stage, batch)[0].start()
            elif kind == 0:
                sum_out(batch)
            else:

                @pl.when(upside == 0)
                def _():
                    cross(1, batch)[0].start()

        def collect(kind, stage, batch):
            copy, mine = exchange(kind, stage, batch)
            copy.wait_recv()
            partial[batch, mine, :] += arrivals[kind][stage][batch]
            follow(kind, stage + 1, batch)

        @pl.when(step == window)
        def _():
            lax.fori_loop(0, window, lambda batch, none: (follow(1, 0, batch), none)[1], 0)

        def within(batch, *more):
            known = jnp.logical_and(batch >= 0, batch < window)
            for condition in more:
                known = jnp.logical_and(known, condition)
            return known

        early = step - window

        @pl.when(within(early, upside == 0))
        def _():
            copy, area = cross(0, early)
            copy.wait_recv()
            partial[early, area, :] += crossed[0][early]
            follow(0, 0, early)

        for stage in range(stages):
            batch = step - window - 2 - stage

            @pl.when(within(batch))
            def _():
                collect(1, stage, batch)

            @pl.when(within(batch, upside == 0))
            def _():
                collect(0, stage, batch)

        late = step - window - 3 - stages

        @pl.when(within(late, upside == 1))
        def _():
            copy, area = cross(1, late)
            copy.wait_recv()
            partial[late, area, :] += crossed[1][late]
            sum_out(late)

        return carry

    lax.fori_loop(0, 2 * window + stages + 3, advance, 0)

    def finish(batch, carry):
        for part in range(SPLITS):
            slot = batch * SPLITS + part

            @pl.when(row < rows - 1)
            def _():
                downward(slot, whole).wait_send()

            @pl.when(col < cols - 1)
            def _():
                rightward(slot, whole).wait_send()

        @pl.when(upside == 1)
        def _():
            cross(0, batch)[0].wait_send()

        @pl.when(upside == 0)
        def _():
            cross(1, batch)[0].wait_send()
            for stage in range(stages):
                exchange(0, stage, batch)[0].wait_send()

        for stage in range(stages):
            exchange(1, stage, batch)[0].wait_send()
        traces_out(batch).wait()
        for part in range(2):
            data_out(batch, part).wait()
        return carry

    lax.fori_loop(0, window, finish, 0)


def local(sources, green, probe, batch_pick, owner_map):
    cols = lax.axis_size("gx")
    rows = lax.axis_size("gz")
    batches, trace, shots = sources.shape[2:]
    window = batch_pick.shape[0]
    receivers = owner_map.shape[1]
    owned = receivers // cols
    group = cols // 2
    stages = group.bit_length() - 1
    slots = window * SPLITS
    half = trace // SPLITS
    total = window * shots
    vmem = pltpu.VMEM
    dma = pltpu.SemaphoreType.DMA
    anywhere = pl.BlockSpec(memory_space=pl.ANY)
    traces, data = pl.pallas_call(
        functools.partial(kernel, cols, rows),
        out_shape=(
            jax.ShapeDtypeStruct((trace, total), jnp.float32),
            jax.ShapeDtypeStruct((2, owned, total), jnp.float32),
        ),
        in_specs=[
            pl.BlockSpec(memory_space=pltpu.SMEM),
            pl.BlockSpec(memory_space=pltpu.VMEM),
            anywhere,
            anywhere,
            anywhere,
        ],
        out_specs=(anywhere, anywhere),
        scratch_shapes=[
            vmem((batches, trace, shots), jnp.float32),
            vmem((max(trace, 2 * receivers), trace), jnp.float32),
            vmem((trace, 2 * trace), jnp.bfloat16),
            vmem((2 * receivers, 2 * trace), jnp.bfloat16),
            vmem((half, shots), jnp.float32),
            vmem((2 * trace, shots), jnp.bfloat16),
            vmem((2 * trace, 2 * shots), jnp.bfloat16),
            vmem((window, trace, shots), jnp.float32),
            vmem((slots, half, shots), jnp.float32),
            vmem((slots, half, shots), jnp.float32),
            vmem((slots, half, shots), jnp.float32),
            vmem((window, 2 * receivers, shots), jnp.float32),
        ]
        + [
            vmem((window, group * 2 * owned, shots), jnp.float32),
            vmem((window, 2 * owned, shots), jnp.float32),
        ]
        + [
            vmem((window, (group >> (stage + 1)) * 2 * owned, shots), jnp.float32)
            for kind in range(2)
            for stage in range(stages)
        ]
        + [
            dma((SPLITS * BLOCKS,)),
            dma(()),
            dma(()),
            dma((slots,)),
            dma((slots,)),
            dma((slots,)),
            dma((slots,)),
            dma((window,)),
            dma((window, 2)),
            dma((2, window)),
            dma((2, window)),
            dma((2, max(stages, 1), window)),
            dma((2, max(stages, 1), window)),
        ],
        compiler_params=pltpu.CompilerParams(
            collective_id=0, has_side_effects=True, vmem_limit_bytes=67043328
        ),
    )(batch_pick, owner_map, sources[0, 0], green[0, 0], probe[0, 0])
    return traces[None, None], data[None]


def solution(mesh):
    return jax.shard_map(
        local,
        mesh=mesh,
        in_specs=(
            P("gz", "gx", None, None, None),
            P("gz", "gx", None, None),
            P("gz", "gx", None, None),
            P(),
            P("gz", None),
        ),
        out_specs=(P("gz", "gx", None, None), P("gz", None, "gx", None)),
        check_vma=False,
    )
```
